32 devices in a mesh: outer: 4 (over y, x), inner: 8 (over z, core).
Axes of the slice: x: 2, y: 2, z: 4, core: 2. Of those that a mesh axis runs over, the one named last changes fastest.
Arguments:
- layer_input: bfloat16 [6144, 8192], P(('outer', 'inner')), may hold values from -6 to 6
- query: bfloat16 [6144, 1024], P(('outer', 'inner')), may hold values from -5 to 5
- keys_values: bfloat16 [6144, 256], P(('outer', 'inner')), may hold values from -5 to 5
- grad_output: bfloat16 [6144, 1024], P(('outer', 'inner')), may hold values from -48 to 48
- logsumexp: float32 [6144, 8], P(('outer', 'inner')), as said below
- delta: float32 [6144, 8], P(('outer', 'inner')), may hold values from -192 to 192
Outputs:
- grad_query: bfloat16 [6144, 1024], P(('outer', 'inner'))
- grad_keys_values: bfloat16 [6144, 256], P(('outer', 'inner'))
- grad_weight: float32 [8192, 256], P('outer')
The draws below stay inside these ranges and needn't reach their ends.
Inputs may be any that keep to these rules, and one draw needn't show every extreme that they name: logsumexp[i, h] exceeds the log-sum-exp of row i's scores over its allowed keys, so that every probs entry is below 1.
All inputs are finite; a program needn't handle non-finite values.
Results may differ from the reference program's by a relative error of at most 0.018.
Values may be sent and summed in bfloat16 or wider, within the bound.
No kernel may reach another device: no remote copies, remote signals or barrier semaphores. Data moves between devices by JAX's collectives and lax.ppermute only.
A program may use at most 64 MiB of HBM per device.

```python
import math
import jax
import jax.numpy as jnp
from jax import lax

D = 8192
HD = 128
HQ = 8
WIN = 3
TOK_DEV = 192
SEGMENT = 1536
TOKENS = 6144
N_OUTER = 4
N_INNER = 8


def joint_draw(key):
    base = jax.random.fold_in(key, 4242)
    key_query, key_kv = jax.random.split(base, 2)
    query_vals = jnp.clip(jax.random.normal(key_query, (TOKENS, HQ * HD), jnp.float32), -4.5, 4.5)
    kv_vals = jnp.clip(jax.random.normal(key_kv, (TOKENS, 2 * HD), jnp.float32), -4.5, 4.5)
    return (query_vals.astype(jnp.bfloat16), kv_vals.astype(jnp.bfloat16))


def window_allowed(tok_rows, inner_pos, outer_pos):
    query_pos = lax.broadcasted_iota(jnp.int32, (tok_rows, (WIN + 2) * tok_rows), 0)
    column = lax.broadcasted_iota(jnp.int32, (tok_rows, (WIN + 2) * tok_rows), 1)
    key_slot = column // tok_rows
    key_pos = column % tok_rows
    own_block = (key_slot == 0) & (key_pos <= query_pos)
    near_block = (key_slot >= 1) & (key_slot <= WIN) & (inner_pos >= key_slot)
    memory_block = (key_slot == WIN + 1) & (outer_pos >= 1)
    return own_block | near_block | memory_block


def draw_query(key, part):
    return joint_draw(key)[0]


def draw_keys_values(key, part):
    return joint_draw(key)[1]


def draw_logsumexp(key, part):
    query_vals, kv_vals = joint_draw(key)
    places = SEGMENT // TOK_DEV
    block_count = TOKENS // TOK_DEV
    query_blocks = query_vals.reshape(block_count, TOK_DEV, HQ, HD).astype(jnp.float32)
    kv_blocks = kv_vals.reshape(block_count, TOK_DEV, 2 * HD)[:, :, :HD].astype(jnp.float32)
    gathered = [kv_blocks]
    for offset in range(1, WIN + 1):
        gathered.append(jnp.roll(kv_blocks, offset, axis=0))
    gathered.append(jnp.roll(kv_blocks, places, axis=0))
    key_rows_all = jnp.concatenate(gathered, axis=1)
    block_ids = jnp.arange(block_count, dtype=jnp.int32)

    def one_block(packed):
        query_blk, key_blk, block_id = packed
        scores = jnp.einsum('thd,kd->thk', query_blk, key_blk) * HD ** (-0.5)
        allowed = window_allowed(TOK_DEV, block_id % places, block_id // places)
        scores = jnp.where(allowed[:, None, :], scores, -jnp.inf)
        return jax.nn.logsumexp(scores, axis=-1)
    window_lse = lax.map(one_block, (query_blocks, key_rows_all, block_ids)).reshape(TOKENS, HQ)
    extra = jnp.exp(jax.random.uniform(jax.random.fold_in(key, 77), (TOKENS, HQ), jnp.float32, math.log(0.1), math.log(3.0)))
    return window_lse + jnp.log1p(extra)


def strengthened(result, rng, source, target, shards_of, factor):
    def block_of(axis_at):
        return (jnp.arange(result.shape[axis_at]) // (result.shape[axis_at] // shards_of)).reshape((-1,) + (1,) * (result.ndim - 1 - axis_at))

    one_side = jax.random.permutation(rng, shards_of)[block_of(target)]
    other_side = (block_of(target) + shards_of // 2) % shards_of
    return jnp.where((block_of(source) == one_side) | (block_of(source) == other_side), factor * result, result)


def level_of(rng, extent, cuts, least, top_value):
    level = 1.0
    for axis_at, shards_of in cuts:
        draws = jax.random.uniform(jax.random.fold_in(jax.random.fold_in(rng, 6), axis_at), (shards_of,), jnp.float32, least / len(cuts), top_value / len(cuts))
        level = level * jnp.repeat(jnp.exp(draws), extent[axis_at] // shards_of).reshape((-1,) + (1,) * (len(extent) - 1 - axis_at))
    return level


def centred(own_key, dims, spread, most, shards=(), kind=jnp.bfloat16):
    factor_of = level_of(own_key, dims, shards, -0.22, 0.18) if shards else 1.0
    values = jax.random.normal(own_key, dims, jnp.float32) * spread * factor_of
    return jnp.minimum(jnp.maximum(values, -most), most).astype(kind)


def bell_draw_with(own_key, dims, width, reach, cuts, heavy, kind=jnp.bfloat16):
    result = width * jax.random.normal(own_key, dims, jnp.float32)
    if cuts:
        result = result * level_of(own_key, dims, cuts, -0.22, 0.18)
    return jnp.clip(strengthened(result, jax.random.fold_in(own_key, 3), *heavy), -reach, reach).astype(kind)


def setup_inputs(seed: int = 0) -> dict:
    key_list = jax.random.split(jax.random.key(seed), 7)
    return {
        "layer_input": bell_draw_with(key_list[0], (TOKENS, D), 1.0, 6.0, ((0, 32),), (0, 1, 32, 2.75)),
        "query": draw_query(jax.random.fold_in(key_list[6], 71), 0),
        "keys_values": draw_keys_values(jax.random.fold_in(key_list[6], 71), 0),
        "grad_output": centred(key_list[3], (TOKENS, HQ * HD), 8.0, 48.0, ((0, 32),)),
        "logsumexp": draw_logsumexp(jax.random.fold_in(key_list[6], 71), 0),
        "delta": centred(key_list[5], (TOKENS, HQ), 32.0, 192.0, ((0, 32),), jnp.float32),
    }


def make_allowed(tok_rows, inner_pos, outer_pos):
    query_pos = lax.broadcasted_iota(jnp.int32, (tok_rows, (WIN + 2) * tok_rows), 0)
    column = lax.broadcasted_iota(jnp.int32, (tok_rows, (WIN + 2) * tok_rows), 1)
    key_slot = column // tok_rows
    key_pos = column % tok_rows
    own_block = (key_slot == 0) & (key_pos <= query_pos)
    near_block = (key_slot >= 1) & (key_slot <= WIN) & (inner_pos >= key_slot)
    memory_block = (key_slot == WIN + 1) & (outer_pos >= 1)
    return own_block | near_block | memory_block


def local_grads(query_blk, key_rows_all, grad_blk, lse_blk, delta_blk, inner_pos, outer_pos):
    tok_rows = query_blk.shape[0]
    scaling = HD ** -0.5
    query_heads = query_blk.reshape(tok_rows, HQ, HD).astype(jnp.float32)
    grad_heads = grad_blk.reshape(tok_rows, HQ, HD).astype(jnp.float32)
    keys_float = key_rows_all[:, :HD].astype(jnp.float32)
    values_float = key_rows_all[:, HD:].astype(jnp.float32)
    scores = jnp.einsum('thd,kd->htk', query_heads, keys_float) * scaling
    allowed = make_allowed(tok_rows, inner_pos, outer_pos)
    scores = jnp.where(allowed[None], scores, -jnp.inf)
    probs = jnp.exp(scores - jnp.transpose(lse_blk)[:, :, None])
    probs_half = probs.astype(jnp.bfloat16)
    grad_probs = jnp.einsum('thd,kd->htk', grad_heads, values_float)
    grad_scores = (probs * (grad_probs - jnp.transpose(delta_blk)[:, :, None]) * scaling).astype(jnp.bfloat16)
    grad_float = grad_scores.astype(jnp.float32)
    grad_query = jnp.einsum('htk,kd->thd', grad_float, keys_float)
    grad_query = grad_query.reshape(tok_rows, HQ * HD).astype(jnp.bfloat16)
    grad_keys = jnp.einsum('htk,thd->kd', grad_float, query_heads)
    grad_values = jnp.einsum('htk,thd->kd', probs_half.astype(jnp.float32), grad_heads)
    return grad_query, jnp.concatenate([grad_keys, grad_values], axis=-1)


def reference(layer_input, query, keys_values, grad_output, logsumexp, delta):
    block_count = N_OUTER * N_INNER
    query_blocks = query.reshape(block_count, TOK_DEV, HQ * HD)
    grad_blocks = grad_output.reshape(block_count, TOK_DEV, HQ * HD)
    lse_blocks = logsumexp.reshape(block_count, TOK_DEV, HQ)
    delta_blocks = delta.reshape(block_count, TOK_DEV, HQ)
    kv_blocks = keys_values.reshape(block_count, TOK_DEV, 2 * HD)
    gathered = [kv_blocks]
    for offset in range(1, WIN + 1):
        gathered.append(jnp.roll(kv_blocks, offset, axis=0))
    gathered.append(jnp.roll(kv_blocks, N_INNER, axis=0))
    key_rows_all = jnp.concatenate(gathered, axis=1)
    block_ids = jnp.arange(block_count, dtype=jnp.int32)

    def one_block(packed):
        query_blk, key_blk, grad_blk, lse_blk, delta_blk, block_id = packed
        return local_grads(query_blk, key_blk, grad_blk, lse_blk, delta_blk, block_id % N_INNER, block_id // N_INNER)

    grad_query, grad_terms = lax.map(one_block, (query_blocks, key_rows_all, grad_blocks, lse_blocks, delta_blocks, block_ids))
    pieces = grad_terms.reshape(block_count, WIN + 2, TOK_DEV, 2 * HD)
    summed = pieces[:, 0]
    for offset in range(1, WIN + 1):
        summed = summed + jnp.roll(pieces[:, offset], -offset, axis=0)
    summed = summed + jnp.roll(pieces[:, WIN + 1], -N_INNER, axis=0)
    grad_kv = summed.astype(jnp.bfloat16)
    input_blocks = layer_input.reshape(block_count, TOK_DEV, D)

    def add_block(running, packed):
        input_blk, grad_blk = packed
        partial_sum = jnp.dot(input_blk.T, grad_blk, preferred_element_type=jnp.float32).astype(jnp.bfloat16)
        partial_sum = lax.optimization_barrier(partial_sum)
        return running + partial_sum.astype(jnp.float32), None

    grad_weight, _ = lax.scan(add_block, jnp.zeros((D, 2 * HD), jnp.float32), (input_blocks, grad_kv))
    return (grad_query.reshape(TOKENS, HQ * HD), grad_kv.reshape(TOKENS, 2 * HD), grad_weight)
```

```python
import functools

import jax
import jax.numpy as jnp
from jax import lax
from jax.experimental import pallas as pl
from jax.experimental.pallas import tpu as pltpu
from jax.sharding import PartitionSpec as P

HD = 128
HQ = 8
WIN = 3
CORES = 2
CHUNKS = 2
LANES = 128


def is_power(count):
    return count & (count - 1) == 0


def target_of(pos, count, step):
    return pos ^ step if is_power(count) else (pos + step) % count


def source_of(pos, count, step):
    return pos ^ step if is_power(count) else (pos - step) % count


def pairs_of(count, step):
    return [(i, target_of(i, count, step)) for i in range(count)]


def rotate(value, axis, steps):
    count = lax.axis_size(axis)
    return lax.ppermute(value, axis, [(i, (i + steps) % count) for i in range(count)])


def across_chips(value, step):
    chips = lax.axis_size("inner") // CORES
    pairs = [(a * CORES + c, b * CORES + c) for a, b in pairs_of(chips, step) for c in range(CORES)]
    return lax.ppermute(value, "inner", pairs)


def swap_cores(value):
    return lax.ppermute(value, "inner", [(i, i ^ 1) for i in range(lax.axis_size("inner"))])


def make_allowed(tok_rows, inner_pos, outer_pos):
    query_pos = lax.broadcasted_iota(jnp.int32, (tok_rows, (WIN + 2) * tok_rows), 0)
    column = lax.broadcasted_iota(jnp.int32, (tok_rows, (WIN + 2) * tok_rows), 1)
    key_slot = column // tok_rows
    key_pos = column % tok_rows
    own_block = (key_slot == 0) & (key_pos <= query_pos)
    near_block = (key_slot >= 1) & (key_slot <= WIN) & (inner_pos >= key_slot)
    memory_block = (key_slot == WIN + 1) & (outer_pos >= 1)
    return own_block | near_block | memory_block


def local_grads(query, key_rows_all, grad_output, logsumexp, delta, inner_pos, outer_pos):
    tok_rows = query.shape[0]
    scaling = HD ** (-0.5)
    query_heads = query.reshape(tok_rows, HQ, HD)
    grad_heads = grad_output.reshape(tok_rows, HQ, HD)
    key_rows = key_rows_all[:, :HD]
    value_rows = key_rows_all[:, HD:]
    scores = (
        jnp.einsum("thd,kd->htk", query_heads, key_rows, preferred_element_type=jnp.float32)
        * scaling
    )
    allowed = make_allowed(tok_rows, inner_pos, outer_pos)
    scores = jnp.where(allowed[None], scores, -jnp.inf)
    probs = jnp.exp(scores - jnp.transpose(logsumexp)[:, :, None])
    probs_half = probs.astype(jnp.bfloat16)
    grad_probs = jnp.einsum(
        "thd,kd->htk", grad_heads, value_rows, preferred_element_type=jnp.float32
    )
    grad_scores = (probs * (grad_probs - jnp.transpose(delta)[:, :, None]) * scaling).astype(
        jnp.bfloat16
    )
    grad_query = jnp.einsum(
        "htk,kd->thd", grad_scores, key_rows, preferred_element_type=jnp.float32
    )
    grad_query = grad_query.reshape(tok_rows, HQ * HD).astype(jnp.bfloat16)
    grad_keys = jnp.einsum(
        "htk,thd->kd", grad_scores, query_heads, preferred_element_type=jnp.float32
    )
    grad_values = jnp.einsum(
        "htk,thd->kd", probs_half, grad_heads, preferred_element_type=jnp.float32
    )
    return (grad_query, jnp.concatenate([grad_keys, grad_values], axis=-1))


def call(body, grid, in_specs, out_specs, out_shape, scalars, *args, flops=0, scratch=()):
    size = sum(a.size * a.dtype.itemsize for a in args)
    return pl.pallas_call(
        body,
        grid_spec=pltpu.PrefetchScalarGridSpec(
            num_scalar_prefetch=1,
            grid=grid,
            in_specs=in_specs,
            out_specs=out_specs,
            scratch_shapes=scratch,
        ),
        out_shape=out_shape,
        compiler_params=pltpu.CompilerParams(vmem_limit_bytes=16 << 20),
        cost_estimate=pl.CostEstimate(flops=flops, transcendentals=0, bytes_accessed=size),
    )(scalars, *args)


def full(shape):
    return pl.BlockSpec(shape, lambda *_: (0,) * len(shape))


def weight_partials(where, mine, theirs, grad, grad_theirs, chunk, width, n_outer):
    rows = mine.shape[0]
    cols = grad.shape[1]
    per_slice = mine.shape[1] // n_outer // width
    per_core = per_slice // CORES

    def body(where_ref, x_ref, y_ref, g_ref, h_ref, *outs):
        step = pl.program_id(0)
        dims = (((0,), (0,)), ((), ()))
        total = lax.dot_general(g_ref[...], x_ref[...], dims, preferred_element_type=jnp.float32)
        total += lax.dot_general(h_ref[...], y_ref[...], dims, preferred_element_type=jnp.float32)
        for k, out in enumerate(outs):

            @pl.when(step == k)
            def _(out=out):
                out[...] = total.astype(out.dtype)

    def block(step, where_ref):
        to = target_of(where_ref[0], n_outer, step)
        return (0, to * per_slice + where_ref[1] * per_core + chunk)

    return call(
        body,
        (n_outer,),
        [pl.BlockSpec((rows, width), block)] * 2 + [full((rows, cols))] * 2,
        [full((cols, width))] * n_outer,
        [jax.ShapeDtypeStruct((cols, width), jnp.float32)]
        + [jax.ShapeDtypeStruct((cols, width), jnp.bfloat16)] * (n_outer - 1),
        where,
        mine,
        theirs,
        grad,
        grad_theirs,
        flops=4 * n_outer * rows * cols * width,
    )


def sum_and_split(where, parts, n_chip, sub):
    cols = parts[0].shape[0]

    def body(where_ref, *refs):
        ins, outs = refs[: len(parts)], refs[len(parts) :]
        step = pl.program_id(0)
        total = ins[0][...].astype(jnp.float32)
        for ref in ins[1:]:
            total += ref[...].astype(jnp.float32)
        for k, out in enumerate(outs):

            @pl.when(step == k)
            def _(out=out):
                out[...] = total.astype(out.dtype)

    def block(step, where_ref):
        return (0, target_of(where_ref[2], n_chip, step))

    return call(
        body,
        (n_chip,),
        [pl.BlockSpec((cols, sub), block)] * len(parts),
        [full((cols, sub))] * n_chip,
        [jax.ShapeDtypeStruct((cols, sub), jnp.float32)]
        + [jax.ShapeDtypeStruct((cols, sub), jnp.bfloat16)] * (n_chip - 1),
        where,
        *parts,
    )


def sum_and_turn(where, parts):
    cols, sub = parts[0].shape

    def body(where_ref, *refs):
        total = refs[0][...]
        for ref in refs[1:-1]:
            total += ref[...].astype(jnp.float32)
        refs[-1][...] = total.T.astype(jnp.bfloat16)

    return call(
        body,
        (1,),
        [full((cols, sub))] * len(parts),
        full((sub, cols)),
        jax.ShapeDtypeStruct((sub, cols), jnp.bfloat16),
        where,
        *parts,
    )


def assemble(where, shards, rows, n_chip, sub):
    cols = shards[0][0][0].shape[1]
    flat = [s for chunk in shards for side in chunk for s in side]
    per_core = rows // CORES

    def body(where_ref, *refs):
        out = refs[-1]
        at = 0
        for j in range(len(shards)):
            for flip in range(CORES):
                for step in range(n_chip):
                    core = where_ref[1] ^ flip
                    chip = source_of(where_ref[2], n_chip, step)
                    start = core * per_core + j * (n_chip * sub) + chip * sub
                    start = pl.multiple_of(start, sub)
                    out[pl.ds(start, sub), :] = refs[at][...].astype(jnp.float32)
                    at += 1

    return call(
        body,
        (1,),
        [full((sub, cols))] * len(flat),
        full((rows, cols)),
        jax.ShapeDtypeStruct((rows, cols), jnp.float32),
        where,
        *flat,
    )


def weight_tiled(layer_input, theirs, grad_kv, grad_theirs, n_outer, n_chip, where):
    rows = layer_input.shape[1] // n_outer
    width = rows // CORES // CHUNKS
    sub = width // n_chip
    sent = []
    for j in range(CHUNKS):
        parts = weight_partials(
            where, layer_input, theirs, grad_kv, grad_theirs, j, width, n_outer
        )
        sent.append(
            [parts[0]]
            + [lax.ppermute(parts[k], "outer", pairs_of(n_outer, k)) for k in range(1, n_outer)]
        )
    shards = []
    for j in range(CHUNKS):
        parts = sum_and_split(where, sent[j], n_chip, sub)
        parts = [parts[0]] + [across_chips(parts[k], k) for k in range(1, n_chip)]
        shard = sum_and_turn(where, parts)
        mine = [shard] + [across_chips(shard, k) for k in range(1, n_chip)]
        shards.append([mine, [swap_cores(s) for s in mine]])
    return assemble(where, shards, rows, n_chip, sub)


def weight_plain(layer_input, theirs, grad_kv, grad_theirs, n_outer, n_chip, where):
    rows = layer_input.shape[1] // n_outer
    half = rows // CORES
    sub = -(-half // n_chip)
    cols = grad_kv.shape[1]
    dims = (((0,), (0,)), ((), ()))

    def part_of(outer):
        start = outer * rows + where[1] * half
        total = 0.0
        for x, g in ((layer_input, grad_kv), (theirs, grad_theirs)):
            x = lax.dynamic_slice(x, (0, start), (x.shape[0], half))
            total += lax.dot_general(x, g, dims, preferred_element_type=jnp.float32)
        return total

    total = part_of(where[0])
    for k in range(1, n_outer):
        part = part_of(target_of(where[0], n_outer, k)).astype(jnp.bfloat16)
        total += lax.ppermute(part, "outer", pairs_of(n_outer, k)).astype(jnp.float32)
    total = jnp.pad(total, ((0, n_chip * sub - half), (0, 0)))
    own = lax.dynamic_slice(total, (where[2] * sub, 0), (sub, cols))
    for k in range(1, n_chip):
        part = lax.dynamic_slice(total, (target_of(where[2], n_chip, k) * sub, 0), (sub, cols))
        own += across_chips(part.astype(jnp.bfloat16), k).astype(jnp.float32)
    shard = own.astype(jnp.bfloat16)
    mine = jnp.zeros((n_chip, sub, cols), jnp.bfloat16)
    mine = lax.dynamic_update_index_in_dim(mine, shard, where[2], 0)
    for k in range(1, n_chip):
        source = source_of(where[2], n_chip, k)
        mine = lax.dynamic_update_index_in_dim(mine, across_chips(shard, k), source, 0)
    mine = mine.reshape(n_chip * sub, cols)[:half]
    other = swap_cores(mine)
    first = jnp.where(where[1] == 0, mine, other)
    second = jnp.where(where[1] == 0, other, mine)
    return jnp.concatenate([first, second], axis=0).astype(jnp.float32)


def local(layer_input, query, keys_values, grad_output, logsumexp, delta):
    tok_rows = query.shape[0]
    n_inner = lax.axis_size("inner")
    n_outer = lax.axis_size("outer")
    n_chip = n_inner // CORES
    inner_pos = lax.axis_index("inner")
    outer_pos = lax.axis_index("outer")
    where = jnp.stack([outer_pos, inner_pos % CORES, inner_pos // CORES]).astype(jnp.int32)
    blocks = [keys_values] + [rotate(keys_values, "inner", w) for w in range(1, WIN + 1)]
    memory = rotate(keys_values, "outer", 1)
    theirs = swap_cores(layer_input)
    key_rows_all = jnp.concatenate(blocks + [memory], axis=0)
    grad_query, grad_terms = local_grads(
        query, key_rows_all, grad_output, logsumexp, delta, inner_pos, outer_pos
    )
    pieces = grad_terms.reshape(WIN + 2, tok_rows, 2 * HD)
    half = pieces[1:].astype(jnp.bfloat16)
    summed = pieces[0]
    for w in range(WIN, 0, -1):
        summed = summed + rotate(half[w - 1], "inner", -w).astype(jnp.float32)
    summed = summed + rotate(half[WIN], "outer", -1).astype(jnp.float32)
    grad_kv = summed.astype(jnp.bfloat16)
    grad_theirs = swap_cores(grad_kv)
    rows = layer_input.shape[1] // n_outer
    tiled = rows % (CORES * CHUNKS * n_chip * LANES) == 0
    product = weight_tiled if tiled else weight_plain
    grad_weight = product(layer_input, theirs, grad_kv, grad_theirs, n_outer, n_chip, where)
    return (grad_query, grad_kv, grad_weight)


def solution(mesh):
    return jax.shard_map(
        local,
        mesh=mesh,
        in_specs=(P(("outer", "inner"), None),) * 6,
        out_specs=(P(("outer", "inner"), None), P(("outer", "inner"), None), P("outer", None)),
        check_vma=False,
    )
```
